32 devices in a mesh: lon: 8 (over z, core), lat: 4 (over y, x).
Axes of the slice: x: 2, y: 2, z: 4, core: 2. Of those that a mesh axis runs over, the one named last changes fastest.
Arguments:
- state: bfloat16 [96, 384, 512], P('lat', 'lon'), may hold values from -6 to 6
- attention_in: bfloat16 [2, 512, 1536], replicated, may hold values from -10 to 10
- attention_out: bfloat16 [2, 512, 512], replicated, may hold values from -0.25 to 0.25
- expand_weight: bfloat16 [2, 512, 2048], replicated, may hold values from -0.25 to 0.25
- depth_kernel: bfloat16 [2, 7, 7, 2048], replicated, may hold values from -0.875 to 0.875
- shrink_weight: bfloat16 [2, 2048, 512], replicated, may hold values from -0.125 to 0.125
- norm_attention: float32 [2, 512], replicated, may hold values from 0.1 to 1.9
- norm_feedforward: float32 [2, 512], replicated, may hold values from 0.1 to 1.9
Outputs:
- advanced_state: bfloat16 [96, 384, 512], P('lat', 'lon')
The draws below stay inside these ranges and needn't reach their ends.
All inputs are finite; a program needn't handle non-finite values.
Results may differ from the reference program's by a relative error of at most 0.009.
Values may be sent and summed in bfloat16 or wider, within the bound.
A program may use at most 128 MiB of HBM per device.

```python
import math
import jax
import jax.numpy as jnp
from jax import lax

D = 512
HEADS = 8
HEAD_DIM = 64
FF = 2048
RADIUS = 6
CONV_RADIUS = 3
LAYERS = 2
KERNEL = 7
NLAT = 96
NLON = 384


def draw_state(key, part):
    own_key = jax.random.fold_in(key, 71)
    first = jax.random.fold_in(own_key, 0)
    extent = (NLAT, NLON, D)
    base = jax.random.normal(first, extent, jnp.float32)
    return jnp.clip(base, -6.0, 6.0).astype(jnp.bfloat16)


def draw_attention_in(key, part):
    own_key = jax.random.fold_in(key, 72)
    first = jax.random.fold_in(own_key, 0)
    base = jnp.clip(jax.random.normal(first, (LAYERS, D, 3 * D), jnp.float32), -5.0, 5.0) * D ** (-0.5)
    return base.astype(jnp.bfloat16)


def noise(rng, shape, width, limit, held_as=jnp.bfloat16):
    return jnp.clip(width * jax.random.normal(rng, shape, jnp.float32), -limit, limit).astype(held_as)


def setup_inputs(seed: int = 0) -> dict:
    seeds = jax.random.split(jax.random.key(seed), 9)
    return {
        "state": draw_state(jax.random.fold_in(seeds[8], 71), 0),
        "attention_in": draw_attention_in(jax.random.fold_in(seeds[8], 71), 0),
        "attention_out": noise(seeds[2], (LAYERS, D, D), D ** -0.5, 0.25),
        "expand_weight": noise(seeds[3], (LAYERS, D, FF), D ** -0.5, 0.25),
        "depth_kernel": noise(seeds[4], (LAYERS, KERNEL, KERNEL, FF), (KERNEL * KERNEL) ** -0.5, 0.875),
        "shrink_weight": noise(seeds[5], (LAYERS, FF, D), FF ** -0.5, 0.125),
        "norm_attention": jnp.clip(1.0 + 0.18 * jax.random.normal(seeds[6], (LAYERS, D), jnp.float32), 0.1, 1.9),
        "norm_feedforward": jnp.clip(1.0 + 0.18 * jax.random.normal(seeds[7], (LAYERS, D), jnp.float32), 0.1, 1.9),
    }


def normalize(stream, gain):
    average = lax.optimization_barrier(jnp.mean(stream, axis=-1, keepdims=True))
    centred = stream - average
    spread = lax.optimization_barrier(jnp.mean(centred * centred, axis=-1, keepdims=True))
    return (centred * lax.rsqrt(spread + 1e-05) * gain.astype(jnp.float32)).astype(jnp.bfloat16)

def widen(field, reach):
    wrapped = jnp.concatenate([field[:, -reach:], field, field[:, :reach]], axis=1)
    return jnp.pad(wrapped, ((reach, reach), (0, 0), (0, 0)))

def attend_global(queries, keys, values):
    height, breadth, channels = queries.shape
    reach = RADIUS
    span = 2 * RADIUS + 1
    key_pad = widen(keys, reach)
    value_pad = widen(values, reach)
    latitudes = jnp.arange(height, dtype=jnp.int32)
    query_heads = queries.astype(jnp.float32).reshape(height, breadth, HEADS, HEAD_DIM)
    scale = 1.0 / math.sqrt(HEAD_DIM)
    offsets = jnp.arange(span * span, dtype=jnp.int32)
    anchor = jnp.zeros((), jnp.int32)

    def score_step(carry, offset):
        down_shift = offset // span
        east_shift = offset % span
        moved = lax.dynamic_slice(key_pad, (down_shift, east_shift, anchor), (height, breadth, channels))
        scores = lax.optimization_barrier(jnp.sum(query_heads * moved.astype(jnp.float32).reshape(height, breadth, HEADS, HEAD_DIM), axis=-1)) * scale
        inside = (latitudes + down_shift - reach >= 0) & (latitudes + down_shift - reach < height)
        return (carry, jnp.where(inside[:, None, None], scores, -jnp.inf))
    unused, scores = lax.scan(score_step, jnp.zeros((), jnp.float32), offsets)
    peak = lax.optimization_barrier(jnp.max(scores, axis=0, keepdims=True))
    expos = jnp.exp(scores - peak)
    weights = (expos / lax.optimization_barrier(jnp.sum(expos, axis=0, keepdims=True))).astype(jnp.bfloat16)

    def value_step(total, item):
        offset, weight = item
        down_shift = offset // span
        east_shift = offset % span
        moved = lax.dynamic_slice(value_pad, (down_shift, east_shift, anchor), (height, breadth, channels))
        moved = moved.astype(jnp.float32).reshape(height, breadth, HEADS, HEAD_DIM)
        return (total + weight.astype(jnp.float32)[..., None] * moved, None)
    start = jnp.zeros((height, breadth, HEADS, HEAD_DIM), jnp.float32)
    total, unused = lax.scan(value_step, start, (offsets, weights))
    return total.reshape(height * breadth, channels).astype(jnp.bfloat16)

def convolve(hidden, kernel):
    height, breadth, units = hidden.shape
    wide = widen(hidden, CONV_RADIUS)
    total = jnp.zeros((height, breadth, units), jnp.float32)
    for down_shift in range(2 * CONV_RADIUS + 1):
        for east_shift in range(2 * CONV_RADIUS + 1):
            piece = wide[down_shift:down_shift + height, east_shift:east_shift + breadth]
            total = total + piece.astype(jnp.float32) * kernel[down_shift, east_shift].astype(jnp.float32)
    return total

def reference(state, attention_in, attention_out, expand_weight, depth_kernel, shrink_weight, norm_attention, norm_feedforward):
    height, breadth, channels = state.shape
    stream = state.astype(jnp.float32).reshape(height * breadth, channels)
    for layer in range(LAYERS):
        normed = normalize(stream, norm_attention[layer])
        weight_in = attention_in[layer]
        queries = jnp.dot(normed, weight_in[:, :channels], preferred_element_type=jnp.float32).astype(jnp.bfloat16)
        keys = jnp.dot(normed, weight_in[:, channels:2 * channels], preferred_element_type=jnp.float32).astype(jnp.bfloat16)
        values = jnp.dot(normed, weight_in[:, 2 * channels:], preferred_element_type=jnp.float32).astype(jnp.bfloat16)
        shape_grid = (height, breadth, channels)
        mixed = attend_global(queries.reshape(shape_grid), keys.reshape(shape_grid), values.reshape(shape_grid))
        stream = stream + jnp.dot(mixed, attention_out[layer], preferred_element_type=jnp.float32)
        normed_ff = normalize(stream, norm_feedforward[layer])
        hidden = jnp.dot(normed_ff, expand_weight[layer], preferred_element_type=jnp.float32).astype(jnp.bfloat16)
        convolved = convolve(hidden.reshape(height, breadth, -1), depth_kernel[layer])
        activated = jax.nn.gelu(convolved, approximate=False).astype(jnp.bfloat16).reshape(height * breadth, -1)
        stream = stream + jnp.dot(activated, shrink_weight[layer], preferred_element_type=jnp.float32)
    return stream.astype(jnp.bfloat16).reshape(height, breadth, channels)
```

```python
import functools
import math

import jax
import jax.numpy as jnp
import numpy as np
from jax import lax
from jax.experimental import pallas as pl
from jax.experimental.pallas import tpu as pltpu
from jax.sharding import PartitionSpec as P

HEADS = 8
HEAD_DIM = 64
RADIUS = 6
CONV_RADIUS = 3
LAYERS = 2
Q_LAT = 4
Q_LON = 16
K_LAT = Q_LAT + 2 * RADIUS
K_LON = 32
GROUP = 4
NEG = -1e30
VMEM_LIMIT = 60 * 1024 * 1024
F32 = jnp.float32
BF16 = jnp.bfloat16


def with_halo(shard, sides, width, wrap):
    for axis, dim in sides:
        peers, length = (lax.axis_size(axis), shard.shape[dim])
        up = [(i, (i + 1) % peers) for i in range(peers if wrap else peers - 1)]
        down = [(j, i) for i, j in up]
        last = lax.slice_in_dim(shard, length - width, length, axis=dim)
        leading = lax.slice_in_dim(shard, 0, width, axis=dim)
        before = lax.ppermute(last, axis, up)
        after = lax.ppermute(leading, axis, down)
        parts = [before, shard, after]
        if dim == 1:
            extra = -(length + 2 * width) % 16
            parts.append(jnp.zeros((shard.shape[0], extra, shard.shape[2]), shard.dtype))
        shard = jnp.concatenate(parts, axis=dim)
    return shard


def halo(tile, width):
    tile = with_halo(tile, (("lat", 0),), width, False)
    return with_halo(tile, (("lon", 1),), width, True)


def norm_rows(stream, gain):
    average = jnp.mean(stream, axis=-1, keepdims=True)
    centred = stream - average
    spread = jnp.mean(centred * centred, axis=-1, keepdims=True)
    return (centred * lax.rsqrt(spread + 1e-05) * gain).astype(BF16)


def erf(x):
    x = jnp.clip(x, -3.832506856900711, 3.832506856900711)
    s = x * x
    a = (
        0.00022905065861350646,
        0.0034082910107109506,
        0.050955695062380861,
        0.18520832239976145,
        1.128379143519084,
    )
    b = (
        -1.1791602954361697e-7,
        0.000023547966471313185,
        0.0010179625278914885,
        0.014070470171167667,
        0.11098505178285362,
        0.49746925110067538,
        1.0,
    )
    top = jnp.full_like(x, a[0])
    for value in a[1:]:
        top = top * s + value
    low = jnp.full_like(x, b[0])
    for value in b[1:]:
        low = low * s + value
    return x * top / low


def gelu(x):
    return 0.5 * x * (1.0 + lax.erf(x * math.sqrt(0.5)))


def attention_kernel(
    own_ref, ext_ref, win_ref, wout_ref, bias_ref, stream_ref, gain_ref,
    out_ref, normed_ref, q_ref, kv_ref, mixed_ref,
):
    height, width, channels = own_ref.shape
    rows, wide, _ = ext_ref.shape
    span = GROUP * HEAD_DIM
    part = Q_LAT * Q_LON

    @pl.loop(0, rows // 4)
    def _(r):
        x = ext_ref[pl.ds(r * 4, 4)].reshape(4 * wide, channels)
        y = jnp.dot(x, win_ref[:, channels:], preferred_element_type=F32)
        kv_ref[pl.ds(r * 4, 4)] = y.astype(BF16).reshape(4, wide, 2 * channels)

    @pl.loop(0, height // 4)
    def _(r):
        x = own_ref[pl.ds(r * 4, 4)].reshape(4 * width, channels)
        y = jnp.dot(x, win_ref[:, :channels], preferred_element_type=F32)
        y = y.astype(BF16) * (1.0 / math.sqrt(HEAD_DIM))
        q_ref[pl.ds(r * 4, 4)] = y.astype(BF16).reshape(4, width, channels)

    lane_head = lax.broadcasted_iota(jnp.int32, (part, span), 1) // HEAD_DIM

    def block(index, carry):
        lat = index // (width // Q_LON)
        lon = index % (width // Q_LON)
        r0 = lat * Q_LAT
        c0 = pl.multiple_of(lon * Q_LON, Q_LON)
        bias = bias_ref[lat]
        for g in range(channels // span):
            lo = g * span
            q = q_ref[pl.ds(r0, Q_LAT), pl.ds(c0, Q_LON), lo : lo + span].reshape(part, span)
            k = kv_ref[pl.ds(r0, K_LAT), pl.ds(c0, K_LON), lo : lo + span]
            v = kv_ref[
                pl.ds(r0, K_LAT), pl.ds(c0, K_LON), channels + lo : channels + lo + span
            ]
            k = k.reshape(K_LAT * K_LON, span)
            v = v.reshape(K_LAT * K_LON, span)
            qq = jnp.concatenate(
                [jnp.where(lane_head == h, q, jnp.zeros_like(q)) for h in range(GROUP)], axis=0
            )
            s = lax.dot_general(qq, k, (((1,), (1,)), ((), ())), preferred_element_type=F32)
            s = (s.reshape(GROUP, part, K_LAT * K_LON) + bias[None]).reshape(s.shape)
            peak = jnp.max(s, axis=-1, keepdims=True)
            e = jnp.exp(s - peak)
            total = jnp.sum(e, axis=-1, keepdims=True)
            o = jnp.dot(e.astype(BF16), v, preferred_element_type=F32) * (1.0 / total)
            m = jnp.zeros((part, span), F32)
            for h in range(GROUP):
                m = jnp.where(lane_head == h, o[h * part : (h + 1) * part], m)
            mixed_ref[pl.ds(r0, Q_LAT), pl.ds(c0, Q_LON), lo : lo + span] = m.astype(
                BF16
            ).reshape(Q_LAT, Q_LON, span)
        return carry

    lax.fori_loop(0, (height // Q_LAT) * (width // Q_LON), block, 0)

    @pl.loop(0, height // 4)
    def _(r):
        x = mixed_ref[pl.ds(r * 4, 4)].reshape(4 * width, channels)
        y = jnp.dot(x, wout_ref[...], preferred_element_type=F32)
        y = y + stream_ref[pl.ds(r * 4, 4)].reshape(4 * width, channels)
        out_ref[pl.ds(r * 4, 4)] = y.reshape(4, width, channels)
        normed_ref[pl.ds(r * 4, 4)] = norm_rows(y, gain_ref[...]).reshape(4, width, channels)


def feed_kernel(last, ext_ref, expand_ref, taps_ref, shrink_ref, stream_ref, gain_ref, *refs):
    if last:
        out_ref, hid_ref, act_ref, acc_ref = refs
    else:
        out_ref, normed_ref, hid_ref, act_ref, acc_ref = refs
    height, width, channels = stream_ref.shape
    rows, wide, _ = ext_ref.shape
    chunk = expand_ref.shape[1]
    side = 2 * CONV_RADIUS + 1
    step = pl.program_id(0)

    @pl.loop(0, rows // 5)
    def _(r):
        x = ext_ref[pl.ds(r * 5, 5)].reshape(5 * wide, channels)
        y = jnp.dot(x, expand_ref[...], preferred_element_type=F32)
        hid_ref[pl.ds(r * 5, 5)] = y.astype(BF16).reshape(5, wide, chunk)

    parts = chunk // 128

    def conv_row(n, carry):
        i = n // parts
        lanes = pl.ds(pl.multiple_of((n % parts) * 128, 128), 128)
        lines = [hid_ref[i + a, :, lanes].reshape(wide // 16, 16, 128) for a in range(side)]
        total = None
        for b in range(side):
            p = lines[0] * taps_ref[0, b, :, lanes]
            for a in range(1, side):
                p = p + lines[a] * taps_ref[a, b, :, lanes]
            p = p.reshape(wide, 128).astype(F32)[b : b + width]
            total = p if total is None else total + p
        act_ref[i, :, lanes] = gelu(total).astype(BF16)
        return carry

    lax.fori_loop(0, height * parts, conv_row, 0)

    @pl.loop(0, height // 4)
    def _(r):
        x = act_ref[pl.ds(r * 4, 4)].reshape(4 * width, chunk)
        y = jnp.dot(x, shrink_ref[...], preferred_element_type=F32)
        rs = pl.ds(r * 4, 4)

        @pl.when(step == 0)
        def _():
            acc_ref[rs] = stream_ref[rs] + y.reshape(4, width, channels)

        @pl.when(step > 0)
        def _():
            acc_ref[rs] = acc_ref[rs] + y.reshape(4, width, channels)

    @pl.when(step == pl.num_programs(0) - 1)
    def _():
        @pl.loop(0, height // 4)
        def _(r):
            rs = pl.ds(r * 4, 4)
            y = acc_ref[rs]
            out_ref[rs] = y.astype(out_ref.dtype)
            if not last:
                z = norm_rows(y.reshape(4 * width, channels), gain_ref[...])
                normed_ref[rs] = z.reshape(4, width, channels)


def full(shape):
    return pl.BlockSpec(shape, lambda *_: (0,) * len(shape))


def attention(own, ext, w_in, w_out, bias, stream, gain):
    shape = own.shape
    height, width, channels = shape
    args = (own, ext, w_in, w_out, bias, stream, gain)
    return pl.pallas_call(
        attention_kernel,
        out_shape=(jax.ShapeDtypeStruct(shape, F32), jax.ShapeDtypeStruct(shape, BF16)),
        in_specs=[pl.BlockSpec(memory_space=pltpu.VMEM)] * len(args),
        out_specs=(pl.BlockSpec(memory_space=pltpu.VMEM),) * 2,
        scratch_shapes=[
            pltpu.VMEM(shape, BF16),
            pltpu.VMEM(ext.shape[:2] + (2 * channels,), BF16),
            pltpu.VMEM(shape, BF16),
        ],
        compiler_params=pltpu.CompilerParams(vmem_limit_bytes=VMEM_LIMIT),
        name="attend",
    )(*args)


def feed(last, ext, expand, taps, shrink, stream, gain):
    shape = stream.shape
    height, width, channels = shape
    units = expand.shape[1]
    chunk = min(512, units)
    side = 2 * CONV_RADIUS + 1
    out_shape = [jax.ShapeDtypeStruct(shape, BF16 if last else F32)]
    if not last:
        out_shape.append(jax.ShapeDtypeStruct(shape, BF16))
    return pl.pallas_call(
        functools.partial(feed_kernel, last),
        out_shape=out_shape,
        grid=(units // chunk,),
        in_specs=[
            full(ext.shape),
            pl.BlockSpec((channels, chunk), lambda j: (0, j)),
            pl.BlockSpec((side, side, 16, chunk), lambda j: (0, 0, 0, j)),
            pl.BlockSpec((chunk, channels), lambda j: (j, 0)),
            full(shape),
            full(gain.shape),
        ],
        out_specs=[full(shape) for _ in out_shape],
        scratch_shapes=[
            pltpu.VMEM(ext.shape[:2] + (chunk,), BF16),
            pltpu.VMEM((height, width, chunk), BF16),
            pltpu.VMEM(shape, F32),
        ],
        compiler_params=pltpu.CompilerParams(vmem_limit_bytes=VMEM_LIMIT),
        name="feed",
    )(ext, expand, taps, shrink, stream, gain)


def score_bias(tile_height):
    band = lax.axis_index("lat")
    grid_height = tile_height * lax.axis_size("lat")
    qi, qj = np.arange(Q_LAT), np.arange(Q_LON)
    ki, kj = np.arange(K_LAT), np.arange(K_LON)
    near_lat = np.abs(ki[None, :] - RADIUS - qi[:, None]) <= RADIUS
    near_lon = np.abs(kj[None, :] - RADIUS - qj[:, None]) <= RADIUS
    starts = np.arange(tile_height // Q_LAT) * Q_LAT
    place = band * tile_height + starts[:, None] + ki[None, :] - RADIUS
    inside = (place >= 0) & (place < grid_height)
    ok_lat = near_lat[None] & inside[:, None, :]
    ok = ok_lat[:, :, None, :, None] & near_lon[None, None, :, None, :]
    bias = jnp.where(ok, 0.0, NEG).astype(F32)
    return bias.reshape(len(starts), Q_LAT * Q_LON, K_LAT * K_LON)


def per_device(
    state,
    attention_in,
    attention_out,
    expand_weight,
    depth_kernel,
    shrink_weight,
    norm_attention,
    norm_feedforward,
):
    bias = score_bias(state.shape[0])
    stream = state.astype(F32)
    normed = norm_rows(stream, norm_attention[0])
    for layer in range(LAYERS):
        last = layer == LAYERS - 1
        taps = depth_kernel[layer]
        taps = jnp.broadcast_to(taps[:, :, None, :], taps.shape[:2] + (16, taps.shape[2]))
        stream, normed_ff = attention(
            normed,
            halo(normed, RADIUS),
            attention_in[layer],
            attention_out[layer],
            bias,
            stream,
            norm_feedforward[layer][None],
        )
        outs = feed(
            last,
            halo(normed_ff, CONV_RADIUS),
            expand_weight[layer],
            taps,
            shrink_weight[layer],
            stream,
            norm_attention[min(layer + 1, LAYERS - 1)][None],
        )
        if last:
            return outs[0]
        stream, normed = outs


def solution(mesh):
    in_specs = (P("lat", "lon", None), P(), P(), P(), P(), P(), P(), P())
    out_specs = P("lat", "lon", None)
    return jax.shard_map(
        per_device, mesh=mesh, in_specs=in_specs, out_specs=out_specs, check_vma=False
    )
```

```python
import functools
import math

import jax
import jax.numpy as jnp
import numpy as np
from jax import lax
from jax.experimental import pallas as pl
from jax.experimental.pallas import tpu as pltpu
from jax.sharding import PartitionSpec as P

HEADS = 8
HEAD_DIM = 64
RADIUS = 6
CONV_RADIUS = 3
LAYERS = 2
Q_LAT = 4
Q_LON = 16
K_LAT = Q_LAT + 2 * RADIUS
K_LON = 32
GROUP = 4
LANES = 256
NEG = -1e30
VMEM_LIMIT = 60 * 1024 * 1024
F32 = jnp.float32
BF16 = jnp.bfloat16


def with_halo(shard, sides, width, wrap):
    for axis, dim in sides:
        peers, length = (lax.axis_size(axis), shard.shape[dim])
        up = [(i, (i + 1) % peers) for i in range(peers if wrap else peers - 1)]
        down = [(j, i) for i, j in up]
        last = lax.slice_in_dim(shard, length - width, length, axis=dim)
        leading = lax.slice_in_dim(shard, 0, width, axis=dim)
        before = lax.ppermute(last, axis, up)
        after = lax.ppermute(leading, axis, down)
        parts = [before, shard, after]
        if dim == 1:
            extra = -(length + 2 * width) % 16
            parts.append(jnp.zeros((shard.shape[0], extra, shard.shape[2]), shard.dtype))
        shard = jnp.concatenate(parts, axis=dim)
    return shard


def halo(tile, width):
    tile = with_halo(tile, (("lat", 0),), width, False)
    return with_halo(tile, (("lon", 1),), width, True)


def norm_rows(stream, gain):
    average = jnp.mean(stream, axis=-1, keepdims=True)
    centred = stream - average
    spread = jnp.mean(centred * centred, axis=-1, keepdims=True)
    return (centred * lax.rsqrt(spread + 1e-05) * gain).astype(BF16)


def erf(x):
    x = jnp.clip(x, -3.832506856900711, 3.832506856900711)
    s = x * x
    a = (
        0.00022905065861350646,
        0.0034082910107109506,
        0.050955695062380861,
        0.18520832239976145,
        1.128379143519084,
    )
    b = (
        -1.1791602954361697e-7,
        0.000023547966471313185,
        0.0010179625278914885,
        0.014070470171167667,
        0.11098505178285362,
        0.49746925110067538,
        1.0,
    )
    top = jnp.full_like(x, a[0])
    for value in a[1:]:
        top = top * s + value
    low = jnp.full_like(x, b[0])
    for value in b[1:]:
        low = low * s + value
    return x * top / low


def gelu(x):
    return 0.5 * x * (1.0 + lax.erf(x * math.sqrt(0.5)))


def attention_kernel(
    own_ref, ext_ref, win_ref, wout_ref, bias_ref, stream_ref, gain_ref,
    out_ref, normed_ref, q_ref, kv_ref, mixed_ref,
):
    height, width, channels = own_ref.shape
    rows, wide, _ = ext_ref.shape
    span = GROUP * HEAD_DIM
    part = Q_LAT * Q_LON

    @pl.loop(0, rows // 4)
    def _(r):
        x = ext_ref[pl.ds(r * 4, 4)].reshape(4 * wide, channels)
        y = jnp.dot(x, win_ref[:, channels:], preferred_element_type=F32)
        kv_ref[pl.ds(r * 4, 4)] = y.astype(BF16).reshape(4, wide, 2 * channels)

    @pl.loop(0, height // 4)
    def _(r):
        x = own_ref[pl.ds(r * 4, 4)].reshape(4 * width, channels)
        y = jnp.dot(x, win_ref[:, :channels], preferred_element_type=F32)
        y = y.astype(BF16) * (1.0 / math.sqrt(HEAD_DIM))
        q_ref[pl.ds(r * 4, 4)] = y.astype(BF16).reshape(4, width, channels)

    lane_head = lax.broadcasted_iota(jnp.int32, (part, span), 1) // HEAD_DIM

    def block(index, carry):
        lat = index // (width // Q_LON)
        lon = index % (width // Q_LON)
        r0 = lat * Q_LAT
        c0 = pl.multiple_of(lon * Q_LON, Q_LON)
        bias = bias_ref[lat]
        for g in range(channels // span):
            lo = g * span
            q = q_ref[pl.ds(r0, Q_LAT), pl.ds(c0, Q_LON), lo : lo + span].reshape(part, span)
            k = kv_ref[pl.ds(r0, K_LAT), pl.ds(c0, K_LON), lo : lo + span]
            v = kv_ref[
                pl.ds(r0, K_LAT), pl.ds(c0, K_LON), channels + lo : channels + lo + span
            ]
            k = k.reshape(K_LAT * K_LON, span)
            v = v.reshape(K_LAT * K_LON, span)
            qq = jnp.concatenate(
                [jnp.where(lane_head == h, q, jnp.zeros_like(q)) for h in range(GROUP)], axis=0
            )
            s = lax.dot_general(qq, k, (((1,), (1,)), ((), ())), preferred_element_type=F32)
            s = (s.reshape(GROUP, part, K_LAT * K_LON) + bias[None]).reshape(s.shape)
            peak = jnp.max(s, axis=-1, keepdims=True)
            e = jnp.exp(s - peak)
            total = jnp.sum(e, axis=-1, keepdims=True)
            o = jnp.dot(e.astype(BF16), v, preferred_element_type=F32) * (1.0 / total)
            m = jnp.zeros((part, span), F32)
            for h in range(GROUP):
                m = jnp.where(lane_head == h, o[h * part : (h + 1) * part], m)
            mixed_ref[pl.ds(r0, Q_LAT), pl.ds(c0, Q_LON), lo : lo + span] = m.astype(
                BF16
            ).reshape(Q_LAT, Q_LON, span)
        return carry

    lax.fori_loop(0, (height // Q_LAT) * (width // Q_LON), block, 0)

    @pl.loop(0, height // 4)
    def _(r):
        x = mixed_ref[pl.ds(r * 4, 4)].reshape(4 * width, channels)
        y = jnp.dot(x, wout_ref[...], preferred_element_type=F32)
        y = y + stream_ref[pl.ds(r * 4, 4)].reshape(4 * width, channels).astype(F32)
        out_ref[pl.ds(r * 4, 4)] = y.reshape(4, width, channels)
        normed_ref[pl.ds(r * 4, 4)] = norm_rows(y, gain_ref[...]).reshape(4, width, channels)


def feed_kernel(last, ext_ref, expand_ref, taps_ref, shrink_ref, stream_ref, gain_ref, *refs):
    if last:
        out_ref, hid_ref, act_ref, acc_ref = refs
    else:
        out_ref, normed_ref, hid_ref, act_ref, acc_ref = refs
    height, width, channels = stream_ref.shape
    rows, wide, _ = ext_ref.shape
    chunk = expand_ref.shape[1]
    side = 2 * CONV_RADIUS + 1
    reach = -(-(width + side - 1) // 8) * 8
    step = pl.program_id(0)

    @pl.loop(0, rows // 5)
    def _(r):
        x = ext_ref[pl.ds(r * 5, 5)].reshape(5 * wide, channels)
        y = jnp.dot(x, expand_ref[...], preferred_element_type=F32)
        hid_ref[pl.ds(r * 5, 5)] = y.astype(BF16).reshape(5, wide, chunk)

    parts = chunk // LANES

    def conv_row(n, carry):
        i = n // parts
        lanes = pl.ds(pl.multiple_of((n % parts) * LANES, LANES), LANES)
        lines = [hid_ref[i + a, 0:reach, lanes].reshape(reach // 8, 8, LANES) for a in range(side)]
        total = None
        for b in range(side):
            p = lines[0] * taps_ref[0, b, :, lanes]
            for a in range(1, side):
                p = p + lines[a] * taps_ref[a, b, :, lanes]
            p = p.reshape(reach, LANES).astype(F32)[b : b + width]
            total = p if total is None else total + p
        act_ref[i, :, lanes] = gelu(total).astype(BF16)
        return carry

    lax.fori_loop(0, height * parts, conv_row, 0)

    @pl.loop(0, height // 4)
    def _(r):
        x = act_ref[pl.ds(r * 4, 4)].reshape(4 * width, chunk)
        y = jnp.dot(x, shrink_ref[...], preferred_element_type=F32)
        rs = pl.ds(r * 4, 4)

        @pl.when(step == 0)
        def _():
            acc_ref[rs] = stream_ref[rs] + y.reshape(4, width, channels)

        @pl.when(step > 0)
        def _():
            acc_ref[rs] = acc_ref[rs] + y.reshape(4, width, channels)

    @pl.when(step == pl.num_programs(0) - 1)
    def _():
        @pl.loop(0, height // 4)
        def _(r):
            rs = pl.ds(r * 4, 4)
            y = acc_ref[rs]
            out_ref[rs] = y.astype(out_ref.dtype)
            if not last:
                z = norm_rows(y.reshape(4 * width, channels), gain_ref[...])
                normed_ref[rs] = z.reshape(4, width, channels)


def pick(shape, layer):
    rest = shape[1:]
    return pl.BlockSpec((None,) + rest, lambda *_: (layer,) + (0,) * len(rest))


def full(shape):
    return pl.BlockSpec(shape, lambda *_: (0,) * len(shape))


def attention(layer, own, ext, w_in, w_out, bias, stream, gain):
    shape = own.shape
    height, width, channels = shape
    args = (own, ext, w_in, w_out, bias, stream, gain)
    return pl.pallas_call(
        attention_kernel,
        out_shape=(jax.ShapeDtypeStruct(shape, F32), jax.ShapeDtypeStruct(shape, BF16)),
        grid=(1,),
        in_specs=[pick(a.shape, layer) if a is w_in or a is w_out else full(a.shape) for a in args],
        out_specs=(full(shape),) * 2,
        scratch_shapes=[
            pltpu.VMEM(shape, BF16),
            pltpu.VMEM(ext.shape[:2] + (2 * channels,), BF16),
            pltpu.VMEM(shape, BF16),
        ],
        compiler_params=pltpu.CompilerParams(vmem_limit_bytes=VMEM_LIMIT),
        name="attend",
    )(*args)


def feed(last, layer, ext, expand, taps, shrink, stream, gain):
    shape = stream.shape
    height, width, channels = shape
    units = expand.shape[2]
    chunk = min(512, units)
    side = 2 * CONV_RADIUS + 1
    out_shape = [jax.ShapeDtypeStruct(shape, BF16 if last else F32)]
    if not last:
        out_shape.append(jax.ShapeDtypeStruct(shape, BF16))
    return pl.pallas_call(
        functools.partial(feed_kernel, last),
        out_shape=out_shape,
        grid=(units // chunk,),
        in_specs=[
            full(ext.shape),
            pl.BlockSpec((None, channels, chunk), lambda j: (layer, 0, j)),
            pl.BlockSpec((side, side, 8, chunk), lambda j: (0, 0, 0, j)),
            pl.BlockSpec((None, chunk, channels), lambda j: (layer, j, 0)),
            full(shape),
            full(gain.shape),
        ],
        out_specs=[full(shape) for _ in out_shape],
        scratch_shapes=[
            pltpu.VMEM(ext.shape[:2] + (chunk,), BF16),
            pltpu.VMEM((height, width, chunk), BF16),
            pltpu.VMEM(shape, F32),
        ],
        compiler_params=pltpu.CompilerParams(vmem_limit_bytes=VMEM_LIMIT),
        name="feed",
    )(ext, expand, taps, shrink, stream, gain)


def score_bias(tile_height):
    band = lax.axis_index("lat")
    grid_height = tile_height * lax.axis_size("lat")
    qi, qj = np.arange(Q_LAT), np.arange(Q_LON)
    ki, kj = np.arange(K_LAT), np.arange(K_LON)
    near_lat = np.abs(ki[None, :] - RADIUS - qi[:, None]) <= RADIUS
    near_lon = np.abs(kj[None, :] - RADIUS - qj[:, None]) <= RADIUS
    starts = np.arange(tile_height // Q_LAT) * Q_LAT
    place = band * tile_height + starts[:, None] + ki[None, :] - RADIUS
    inside = (place >= 0) & (place < grid_height)
    ok_lat = near_lat[None] & inside[:, None, :]
    ok = ok_lat[:, :, None, :, None] & near_lon[None, None, :, None, :]
    bias = jnp.where(ok, 0.0, NEG).astype(F32)
    return bias.reshape(len(starts), Q_LAT * Q_LON, K_LAT * K_LON)


def per_device(
    state,
    attention_in,
    attention_out,
    expand_weight,
    depth_kernel,
    shrink_weight,
    norm_attention,
    norm_feedforward,
):
    bias = score_bias(state.shape[0])
    stream = state
    normed = norm_rows(state.astype(F32), norm_attention[0])
    for layer in range(LAYERS):
        last = layer == LAYERS - 1
        taps = depth_kernel[layer]
        taps = jnp.broadcast_to(taps[:, :, None, :], taps.shape[:2] + (8, taps.shape[2]))
        stream, normed_ff = attention(
            layer,
            normed,
            halo(normed, RADIUS),
            attention_in,
            attention_out,
            bias,
            stream,
            norm_feedforward[layer][None],
        )
        outs = feed(
            last,
            layer,
            halo(normed_ff, CONV_RADIUS),
            expand_weight,
            taps,
            shrink_weight,
            stream,
            norm_attention[min(layer + 1, LAYERS - 1)][None],
        )
        if last:
            return outs[0]
        stream, normed = outs


def solution(mesh):
    in_specs = (P("lat", "lon", None), P(), P(), P(), P(), P(), P(), P())
    out_specs = P("lat", "lon", None)
    return jax.shard_map(
        per_device, mesh=mesh, in_specs=in_specs, out_specs=out_specs, check_vma=False
    )
```
